32 devices in a mesh: group: 2 (over x), route: 4 (over y, core), cuts: 4 (over z).
Axes of the slice: x: 2, y: 2, z: 4, core: 2. Of those that a mesh axis runs over, the one named last changes fastest.
Arguments:
- query_matrix_rows: bfloat16 [1024, 4096], P(('group', 'route'), 'cuts'), parts along dimension 0, may hold values from -8 to 8
- key_matrix_rows: bfloat16 [1024, 1024], P(('group', 'route'), 'cuts'), parts along dimension 0, may hold values from -8 to 8
- value_matrix_rows: bfloat16 [1024, 1024], P(('group', 'route'), 'cuts'), parts along dimension 0, may hold values from -6 to 6
- attention_output_matrix: bfloat16 [4096, 4096], P('cuts'), may hold values from -0.125 to 0.125
- residual: bfloat16 [1024, 4096], P(('group', 'route'), 'cuts'), parts along dimension 0, may hold values from -6 to 6
- cotangent: bfloat16 [1024, 4096], P(('group', 'route'), 'cuts'), parts along dimension 0, may hold values from -0.59765625 to 0.59765625
- token_expert_choices: int32 [1024, 2], P(('group', 'route')), parts along dimension 0, may hold values from 0 to 3, as said below
- token_slot_positions: int32 [1024, 2], P(('group', 'route')), parts along dimension 0, may hold values from 0 to 127, as said below
- router_choice_weight: float32 [1024, 2], P(('group', 'route')), parts along dimension 0, may hold values from 0.2 to 1
- expert_gate_weight: bfloat16 [4, 3200, 4096], P('route', 'cuts'), may hold values from -0.09375 to 0.09375
- expert_down_weight: bfloat16 [4, 3200, 4096], P('route', 'cuts'), may hold values from -0.15625 to 0.15625
- adapter_down_factor: bfloat16 [4, 64, 4096], P('route'), may hold values from -0.09375 to 0.09375
- adapter_up_factor: bfloat16 [4, 64, 3200], P('route', None, 'cuts'), may hold values from -0.75 to 0.75
Outputs:
- layer_out: bfloat16 [1024, 4096], P(('group', 'route'), 'cuts'), parts along dimension 0
- down_factor_gradient: float32 [8, 64, 4096], P(('group', 'route'), None, 'cuts'), parts along dimension 0
- up_factor_gradient: float32 [8, 64, 3200], P(('group', 'route'), None, 'cuts'), parts along dimension 0
The draws below stay inside these ranges and needn't reach their ends.
There are 2 independent parts, one for each index of `group`. The reference program is written for one: setup_inputs(seed, part) draws one part's arguments, and reference() takes and returns one part's arrays. A program takes and returns all parts, laid end to end along the dimension named above; an argument that names none is the same for every part. Nothing has to cross between parts.
Inputs may be any that keep to these rules, and one draw needn't show every extreme that they name: `token_expert_choices`: the two experts of a token differ. Within one sequence of 128 tokens no expert is named more than 128 times; one expert, the same for all sequences of a draw, is named exactly 128 times in every sequence. `token_slot_positions`: within one sequence the slots given for one expert are all different.
All inputs are finite; a program needn't handle non-finite values.
Results may differ from the reference program's by a relative error of at most 0.014.
Values may be sent and summed in bfloat16 or wider, within the bound.
No kernel may reach another device: no remote copies, remote signals or barrier semaphores. Data moves between devices by JAX's collectives and lax.ppermute only.
A program may use at most 128 MiB of HBM per device.

```python
import math
import jax
import jax.numpy as jnp
from jax import lax

MODEL_DIMENSION = 4096
HEADS = 32
KV_HEADS = 8
HEAD_DIM = 128
FEEDFORWARD_UNITS = 3200
ADAPTER_RANK = 64
LEN = 128
EXPERT_COUNT = 4
TOKENS = 512
CAP = 128
N_CUTS = 4


def attention_draws(key):
    base_q = jax.random.fold_in(key, 101)
    base_k = jax.random.fold_in(key, 102)
    query_vals = jnp.clip(jax.random.normal(base_q, (TOKENS, HEADS * HEAD_DIM), jnp.float32), -6.0, 6.0)
    key_vals = jnp.clip(jax.random.normal(base_k, (TOKENS, KV_HEADS * HEAD_DIM), jnp.float32), -6.0, 6.0)
    return (query_vals, key_vals)


def draw_query_matrix_rows(key, part):
    return attention_draws(key)[0].astype(jnp.bfloat16)


def draw_key_matrix_rows(key, part):
    return attention_draws(key)[1].astype(jnp.bfloat16)


def routing_draws(key):
    seq_count = TOKENS // LEN
    cell_count = EXPERT_COUNT * CAP
    hot_expert = jax.random.randint(jax.random.fold_in(key, 201), (), 0, EXPERT_COUNT)
    expert_bias = jax.random.randint(jax.random.fold_in(key, 202), (EXPERT_COUNT,), 0, 4 * CAP)

    def per_sequence(seq_key):
        noise_ints = jax.random.randint(jax.random.fold_in(seq_key, 1), (EXPERT_COUNT, CAP), 0, 4 * CAP)
        boost = jnp.where(jnp.arange(EXPERT_COUNT)[:, None] == hot_expert, 16 * CAP, 0)
        scores = noise_ints + expert_bias[:, None] + boost
        unique = scores.reshape(-1) * cell_count + jax.random.permutation(jax.random.fold_in(seq_key, 2), cell_count)
        ranking = jnp.argsort(-unique)
        chosen = jnp.sort(ranking[:2 * LEN])
        first_half = chosen[:LEN]
        second = chosen[LEN:]
        swapped = jax.random.randint(jax.random.fold_in(seq_key, 3), (LEN,), 0, 2) == 1
        paired = jnp.stack([jnp.where(swapped, second, first_half), jnp.where(swapped, first_half, second)], axis=1)
        placing = jax.random.permutation(jax.random.fold_in(seq_key, 4), LEN)
        return paired[jnp.argsort(placing)]
    seq_keys = jax.random.split(jax.random.fold_in(key, 203), seq_count)
    paired = jax.vmap(per_sequence)(seq_keys).reshape(TOKENS, 2)
    return ((paired // CAP).astype(jnp.int32), (paired % CAP).astype(jnp.int32))


def draw_token_expert_choices(key, part):
    return routing_draws(key)[0]


def draw_token_slot_positions(key, part):
    return routing_draws(key)[1]


def strengthened(result, key, source, target, shards_of, factor):
    owner, partner = [(jnp.arange(result.shape[position]) // (result.shape[position] // shards_of)).reshape([-1 if axis == position else 1 for axis in range(result.ndim)]) for position in (source, target)]
    chosen = jax.random.permutation(key, shards_of)[partner]
    strong = (owner == chosen) | (owner == (partner + shards_of // 2) % shards_of)
    return jnp.where(strong, factor * result, result)


def block_scale(key, extent, shards, least, high):
    level = 1.0
    for position, shards_of in shards:
        steps = jax.random.uniform(jax.random.fold_in(jax.random.fold_in(key, 6), position), (shards_of,), jnp.float32, least / len(shards), high / len(shards))
        level = level * jnp.repeat(jnp.exp(steps), extent[position] // shards_of).reshape((-1,) + (1,) * (len(extent) - 1 - position))
    return level


def centred(own_key, dims, deviation, most, cuts=(), kind=jnp.bfloat16):
    values = deviation * jax.random.normal(own_key, dims, jnp.float32)
    if cuts:
        values = values * block_scale(own_key, dims, cuts, -0.22, 0.18)
    return jnp.clip(values, -most, most).astype(kind)


def heavy_noise(own_key, shape, width, limit, pieces, heavy, kind=jnp.bfloat16):
    result = width * jax.random.normal(own_key, shape, jnp.float32)
    if pieces:
        result = result * block_scale(own_key, shape, pieces, -0.22, 0.18)
    return jnp.clip(strengthened(result, jax.random.fold_in(own_key, 3), *heavy), -limit, limit).astype(kind)


def setup_inputs(seed: int = 0, part: int = 0) -> dict:
    arg_keys = jax.random.split(jax.random.key(seed), 14)
    own_keys = jax.random.split(jax.random.fold_in(arg_keys[13], part), 14)
    return {
        "query_matrix_rows": draw_query_matrix_rows(jax.random.fold_in(jax.random.fold_in(arg_keys[13], part), 71), part),
        "key_matrix_rows": draw_key_matrix_rows(jax.random.fold_in(jax.random.fold_in(arg_keys[13], part), 71), part),
        "value_matrix_rows": centred(own_keys[2], (TOKENS, KV_HEADS * HEAD_DIM), 1.0, 6.0, ((0, 4), (1, 4))),
        "attention_output_matrix": heavy_noise(arg_keys[3], (HEADS * HEAD_DIM, MODEL_DIMENSION), (HEADS * HEAD_DIM) ** -0.5, 0.125, ((0, 4),), (0, 1, 4, 2.0)),
        "residual": centred(own_keys[4], (TOKENS, MODEL_DIMENSION), 1.0, 6.0, ((0, 4), (1, 4))),
        "cotangent": centred(own_keys[5], (TOKENS, MODEL_DIMENSION), 0.1, 0.59765625, ((0, 4), (1, 4))),
        "token_expert_choices": draw_token_expert_choices(jax.random.fold_in(jax.random.fold_in(arg_keys[13], part), 71), part),
        "token_slot_positions": draw_token_slot_positions(jax.random.fold_in(jax.random.fold_in(arg_keys[13], part), 71), part),
        "router_choice_weight": jnp.clip(jnp.exp(math.log(1.0) - 1.609438 * jax.random.uniform(own_keys[8], (TOKENS, 2), jnp.float32) ** block_scale(own_keys[8], (TOKENS, 2), ((0, 4),), -0.2, 0.2)), 0.2, 1.0),
        "expert_gate_weight": centred(arg_keys[9], (EXPERT_COUNT, FEEDFORWARD_UNITS, MODEL_DIMENSION), MODEL_DIMENSION ** -0.5, 0.09375, ((0, 4), (1, 4))),
        "expert_down_weight": heavy_noise(arg_keys[10], (EXPERT_COUNT, FEEDFORWARD_UNITS, MODEL_DIMENSION), FEEDFORWARD_UNITS ** -0.5, 0.15625, ((0, 4), (1, 4)), (1, 2, 4, 2.0)),
        "adapter_down_factor": centred(arg_keys[11], (EXPERT_COUNT, ADAPTER_RANK, MODEL_DIMENSION), MODEL_DIMENSION ** -0.5, 0.09375, ((0, 4),)),
        "adapter_up_factor": centred(arg_keys[12], (EXPERT_COUNT, ADAPTER_RANK, FEEDFORWARD_UNITS), ADAPTER_RANK ** -0.5, 0.75, ((0, 4), (2, 4))),
    }


ADAPTER_SCALE = 0.5

def sequence_heads(blocks):
    seq_q, seq_k, seq_v = blocks
    per_kv = HEADS // KV_HEADS
    queries = seq_q.reshape(LEN, KV_HEADS, per_kv, HEAD_DIM).astype(jnp.float32)
    key_view = seq_k.reshape(LEN, KV_HEADS, HEAD_DIM).astype(jnp.float32)
    value_view = seq_v.reshape(LEN, KV_HEADS, HEAD_DIM).astype(jnp.float32)
    scores = jnp.einsum('qhgd,khd->hgqk', queries, key_view) / math.sqrt(HEAD_DIM)
    future = lax.broadcasted_iota(jnp.int32, (LEN, LEN), 1) > lax.broadcasted_iota(jnp.int32, (LEN, LEN), 0)
    scores = jnp.where(future, -jnp.inf, scores)
    row_max = lax.optimization_barrier(jnp.max(scores, axis=-1, keepdims=True))
    shifted = jnp.exp(scores - row_max)
    weights = (shifted / lax.optimization_barrier(jnp.sum(shifted, axis=-1, keepdims=True))).astype(jnp.bfloat16)
    attended = jnp.einsum('hgqk,khd->qhgd', weights.astype(jnp.float32), value_view)
    return attended.astype(jnp.bfloat16).reshape(LEN, HEADS * HEAD_DIM)

def reference(query_matrix_rows, key_matrix_rows, value_matrix_rows, attention_output_matrix, residual, cotangent, token_expert_choices, token_slot_positions, router_choice_weight, expert_gate_weight, expert_down_weight, adapter_down_factor, adapter_up_factor):
    seq_count = TOKENS // LEN
    attended = lax.map(sequence_heads, (query_matrix_rows.reshape(seq_count, LEN, -1), key_matrix_rows.reshape(seq_count, LEN, -1), value_matrix_rows.reshape(seq_count, LEN, -1)))
    attended = attended.reshape(TOKENS, HEADS * HEAD_DIM)
    head_out = jnp.dot(attended, attention_output_matrix, preferred_element_type=jnp.float32)
    hidden = (residual.astype(jnp.float32) + head_out).astype(jnp.bfloat16)
    token_index = jnp.arange(TOKENS, dtype=jnp.int32)
    seq_index = token_index // LEN
    flat_seq = jnp.repeat(seq_index, 2)
    row_pos = (flat_seq * CAP + token_slot_positions.reshape(-1)).astype(jnp.int32)
    owners = jnp.full((EXPERT_COUNT, seq_count * CAP), TOKENS, jnp.int32)
    owners = owners.at[token_expert_choices.reshape(-1), row_pos].set(jnp.repeat(token_index, 2))
    scales = jnp.zeros((EXPERT_COUNT, seq_count * CAP), jnp.float32)
    scales = scales.at[token_expert_choices.reshape(-1), row_pos].set(router_choice_weight.reshape(-1))
    padded_x = jnp.concatenate([hidden, jnp.zeros((1, MODEL_DIMENSION), hidden.dtype)], axis=0)
    padded_g = jnp.concatenate([cotangent, jnp.zeros((1, MODEL_DIMENSION), cotangent.dtype)], axis=0)
    slice_width = FEEDFORWARD_UNITS // N_CUTS

    def expert_step(current_expert):
        expert_input_rows = jnp.take(padded_x, owners[current_expert], axis=0)
        rows_g = (jnp.take(padded_g, owners[current_expert], axis=0).astype(jnp.float32) * scales[current_expert][:, None]).astype(jnp.bfloat16)
        expert_gate_matrix = expert_gate_weight[current_expert]
        down_w = expert_down_weight[current_expert]
        down_factor_slice = adapter_down_factor[current_expert]
        up_factor_slice = adapter_up_factor[current_expert]
        adapter_product = jnp.dot(expert_input_rows, down_factor_slice.T, preferred_element_type=jnp.float32).astype(jnp.bfloat16)
        gate_preactivation = jnp.dot(expert_input_rows, expert_gate_matrix.T, preferred_element_type=jnp.float32) + ADAPTER_SCALE * jnp.dot(adapter_product, up_factor_slice, preferred_element_type=jnp.float32)
        sigmoid_gate = jax.nn.sigmoid(gate_preactivation)
        activ = (gate_preactivation * sigmoid_gate).astype(jnp.bfloat16)
        expert_output_rows = jnp.zeros((expert_input_rows.shape[0], MODEL_DIMENSION), jnp.float32)
        for piece_index in range(N_CUTS):
            lower = piece_index * slice_width
            piece_out = jnp.dot(activ[:, lower:lower + slice_width], down_w[lower:lower + slice_width], preferred_element_type=jnp.float32)
            expert_output_rows = expert_output_rows + piece_out.astype(jnp.bfloat16).astype(jnp.float32)
        grad_hidden = jnp.dot(rows_g, down_w.T, preferred_element_type=jnp.float32)
        preactivation_gradient = (grad_hidden * sigmoid_gate * (1.0 + gate_preactivation * (1.0 - sigmoid_gate))).astype(jnp.bfloat16)
        up_factor_gradient = ADAPTER_SCALE * jnp.dot(adapter_product.T, preactivation_gradient, preferred_element_type=jnp.float32)
        down_factor_gradient = jnp.zeros((ADAPTER_RANK, MODEL_DIMENSION), jnp.float32)
        for piece_index in range(N_CUTS):
            lower = piece_index * slice_width
            factor_part = jnp.dot(preactivation_gradient[:, lower:lower + slice_width], up_factor_slice[:, lower:lower + slice_width].T, preferred_element_type=jnp.float32).astype(jnp.bfloat16)
            down_factor_gradient = down_factor_gradient + jnp.dot(factor_part.T, expert_input_rows, preferred_element_type=jnp.float32)
        return (expert_output_rows, ADAPTER_SCALE * down_factor_gradient, up_factor_gradient)
    outputs, grads_a, grads_b = lax.map(expert_step, jnp.arange(EXPERT_COUNT, dtype=jnp.int32))
    first_out = outputs[token_expert_choices[:, 0], (seq_index * CAP + token_slot_positions[:, 0]).astype(jnp.int32)]
    second_out = outputs[token_expert_choices[:, 1], (seq_index * CAP + token_slot_positions[:, 1]).astype(jnp.int32)]
    picked = router_choice_weight[:, 0:1] * first_out + router_choice_weight[:, 1:2] * second_out
    layer_out = (hidden.astype(jnp.float32) + picked).astype(jnp.bfloat16)
    return (layer_out, grads_a, grads_b)
```

```python
import math

import jax
import jax.numpy as jnp
from jax import lax
from jax.sharding import PartitionSpec as P

HEAD_DIM = 128
ADAPTER_SCALE = 0.5
F32 = jnp.float32
BF16 = jnp.bfloat16
LAST = (((1,), (1,)), ((), ()))
FIRST = (((0,), (0,)), ((), ()))


def causal_heads(query_matrix_rows, key_matrix_rows, value_matrix_rows):
    length = query_matrix_rows.shape[0]
    kv_local = key_matrix_rows.shape[1] // HEAD_DIM
    per_kv = query_matrix_rows.shape[1] // key_matrix_rows.shape[1]
    queries = query_matrix_rows.reshape(length, kv_local, per_kv, HEAD_DIM)
    key_view = key_matrix_rows.reshape(length, kv_local, HEAD_DIM)
    value_view = value_matrix_rows.reshape(length, kv_local, HEAD_DIM)
    scores = jnp.einsum(
        "qhgd,khd->hgqk", queries, key_view, preferred_element_type=jnp.float32
    ) / math.sqrt(HEAD_DIM)
    future = lax.broadcasted_iota(jnp.int32, (length, length), 1) > lax.broadcasted_iota(
        jnp.int32, (length, length), 0
    )
    scores = jnp.where(future, -jnp.inf, scores)
    row_max = jnp.max(scores, axis=-1, keepdims=True)
    shifted = jnp.exp(scores - row_max)
    weights = (shifted / jnp.sum(shifted, axis=-1, keepdims=True)).astype(jnp.bfloat16)
    attended = jnp.einsum("hgqk,khd->qhgd", weights, value_view, preferred_element_type=jnp.float32)
    return attended.astype(jnp.bfloat16).reshape(length, query_matrix_rows.shape[1])


class Line:
    def __init__(self, axis, n, inner=1, core=False):
        self.axis, self.n = axis, n
        self.steps = []
        self.arrivals = [[] for _ in range(n)]
        for k in range(1, n):
            moves = {"a": [], "b": []}
            for i in range(n):
                for j, block in ((i + 1, i - k + 1), (i - 1, i + k - 1)):
                    if 0 <= j < n and 0 <= block < n:
                        kind = "a" if min(i, j) % 2 == 0 else "b"
                        moves[kind].append((i, j))
                        self.arrivals[j].append((k, kind, block))
            self.steps.append((k, moves))
        for row in self.arrivals:
            row.sort()
        if core:
            self.pairs = lambda moves: [
                (p * 2 + i, p * 2 + j) for p in range(lax.axis_size(axis) // 2) for i, j in moves
            ]
            self.index = lambda: lax.axis_index(axis) % 2
        else:
            self.pairs = lambda moves: [
                (i * inner + c, j * inner + c) for i, j in moves for c in range(inner)
            ]
            self.index = lambda: lax.axis_index(axis) // inner

    def blocks(self):
        me = self.index()
        table = [[i] + [block for _, _, block in self.arrivals[i]] for i in range(self.n)]
        return [jnp.array([row[m] for row in table], jnp.int32)[me] for m in range(self.n)]

    def _pick(self, options):
        values = list(options.values())
        out = values[0][0]
        for value, positions in values[1:]:
            mine = jnp.array([i in positions for i in range(self.n)])[self.index()]
            out = jnp.where(mine, value, out)
        return out

    def permute(self, x, moves):
        return lax.ppermute(x, self.axis, self.pairs(moves))

    def gather(self, x):
        got = {(0, "a"): x, (0, "b"): x}
        for k, moves in self.steps:
            for kind, source in (("a", "b"), ("b", "a")):
                if moves[kind]:
                    got[k, kind] = self.permute(got[k - 1, source], moves[kind])
        slots = [x]
        for m in range(self.n - 1):
            options = {}
            for i in range(self.n):
                k, kind, _ = self.arrivals[i][m]
                options.setdefault((k, kind), (got[k, kind], []))[1].append(i)
            slots.append(self._pick(options))
        return slots

    def reduce(self, slots):
        back = {}
        for k, moves in reversed(self.steps):
            for kind, other in (("a", "b"), ("b", "a")):
                if not moves[kind]:
                    continue
                options = {}
                for i in range(self.n):
                    for m, (step, sort, _) in enumerate(self.arrivals[i]):
                        if (step, sort) == (k, kind):
                            options.setdefault(m, (slots[m + 1], []))[1].append(i)
                term = self._pick(options)
                if (k + 1, other) in back:
                    term = (term.astype(F32) + back[k + 1, other].astype(F32)).astype(BF16)
                back[k, kind] = self.permute(
                    term.astype(BF16), [(j, i) for i, j in moves[kind]]
                )
        total = slots[0].astype(F32)
        for kind in ("a", "b"):
            if (1, kind) in back:
                total = total + back[1, kind].astype(F32)
        return total


def column_block(matrix, block, width):
    return lax.dynamic_slice_in_dim(matrix, block * width, width, axis=1)


def dense_layer(
    query_matrix_rows,
    key_matrix_rows,
    value_matrix_rows,
    attention_output_matrix,
    residual,
    cotangent,
    token_expert_choices,
    router_choice_weight,
    expert_gate_weight,
    expert_down_weight,
    adapter_down_factor,
    adapter_up_factor,
):
    length, width = residual.shape
    cuts, route = lax.axis_size("cuts"), lax.axis_size("route")
    inner = 2 if route % 2 == 0 else 1
    zline = Line("cuts", cuts)
    yline = Line("route", route // inner, inner)
    cline = Line("route", inner, core=True) if inner == 2 else None

    def spread(x):
        x = jnp.concatenate(yline.gather(x), axis=0)
        return jnp.concatenate(cline.gather(x), axis=0) if cline else x

    def collect(x):
        if cline:
            x = cline.reduce(jnp.split(x, inner, axis=0)).astype(BF16)
        return yline.reduce(jnp.split(x, route // inner, axis=0)).astype(BF16)

    columns = zline.blocks()
    gate, down = expert_gate_weight[0], expert_down_weight[0]
    low_in, low_out = adapter_down_factor[0], adapter_up_factor[0]

    chosen = token_expert_choices[:, :, None] == jnp.arange(route, dtype=jnp.int32)
    table = jnp.sum(jnp.where(chosen, router_choice_weight[:, :, None], 0.0), axis=1).T
    tables = spread(table[None])
    scale = lax.dynamic_index_in_dim(tables, lax.axis_index("route"), axis=1, keepdims=False)
    scale = scale.reshape(-1, 1)

    cot_slots = [spread(x) for x in zline.gather(cotangent)]

    attended = causal_heads(query_matrix_rows, key_matrix_rows, value_matrix_rows)
    terms = [
        jnp.dot(
            attended,
            column_block(attention_output_matrix, block, width),
            preferred_element_type=F32,
        )
        for block in columns
    ]
    terms = [terms[0]] + [x.astype(BF16) for x in terms[1:]]
    head_cols = zline.reduce(terms)
    hidden = (residual.astype(F32) + head_cols).astype(BF16)

    hid_slots = [spread(x) for x in zline.gather(hidden)]
    pre, low, grad_hidden = 0.0, 0.0, 0.0
    for x, block in zip(hid_slots, columns, strict=True):
        pre += lax.dot_general(x, column_block(gate, block, width), LAST, preferred_element_type=F32)
        low += lax.dot_general(
            x, column_block(low_in, block, width), LAST, preferred_element_type=F32
        )
    low = low.astype(BF16)
    pre = pre + ADAPTER_SCALE * jnp.dot(low, low_out, preferred_element_type=F32)
    sig = jax.nn.sigmoid(pre)
    activ = (pre * sig).astype(BF16)

    outs = [None] * cuts
    for m in reversed(range(cuts)):
        part = jnp.dot(activ, column_block(down, columns[m], width), preferred_element_type=F32)
        outs[m] = collect((scale * part).astype(BF16))
    layer_out = (hidden.astype(F32) + zline.reduce(outs)).astype(BF16)

    for x, block in zip(cot_slots, columns, strict=True):
        grad_hidden += lax.dot_general(
            x, column_block(down, block, width), LAST, preferred_element_type=F32
        )
    grad_pre = (scale * grad_hidden * sig * (1.0 + pre * (1.0 - sig))).astype(BF16)
    up_grad = ADAPTER_SCALE * lax.dot_general(low, grad_pre, FIRST, preferred_element_type=F32)
    factor = lax.dot_general(low_out, grad_pre, LAST, preferred_element_type=F32).astype(BF16)
    total = factor.astype(F32)
    for shift in range(1, cuts):
        total += lax.ppermute(
            factor, "cuts", [(i, (i + shift) % cuts) for i in range(cuts)]
        ).astype(F32)
    down_grad = ADAPTER_SCALE * jnp.dot(
        total.astype(BF16), hid_slots[0], preferred_element_type=F32
    )
    return layer_out, down_grad[None], up_grad[None]


def fill_slots(source_rows, owners):
    padded = jnp.concatenate(
        [source_rows, jnp.zeros((1, source_rows.shape[1]), source_rows.dtype)], axis=0
    )
    return jnp.take(padded, owners, axis=0)


def weighted_slots(source_rows, owners, scales):
    return (fill_slots(source_rows, owners).astype(jnp.float32) * scales[:, None]).astype(
        jnp.bfloat16
    )


def combine_rows(returned, cell_ids, router_choice_weight):
    first_out = jnp.take(returned, cell_ids[:, 0], axis=0)
    second_out = jnp.take(returned, cell_ids[:, 1], axis=0)
    return router_choice_weight[:, 0:1] * first_out + router_choice_weight[:, 1:2] * second_out


def slot_layer(
    query_matrix_rows,
    key_matrix_rows,
    value_matrix_rows,
    attention_output_matrix,
    residual,
    cotangent,
    token_expert_choices,
    token_slot_positions,
    router_choice_weight,
    expert_gate_weight,
    expert_down_weight,
    adapter_down_factor,
    adapter_up_factor,
):
    attended = causal_heads(query_matrix_rows, key_matrix_rows, value_matrix_rows)
    head_terms = jnp.dot(attended, attention_output_matrix, preferred_element_type=jnp.float32)
    head_cols = lax.psum_scatter(head_terms, "cuts", scatter_dimension=1, tiled=True)
    hidden_cols = (residual.astype(jnp.float32) + head_cols).astype(jnp.bfloat16)
    length = residual.shape[0]
    col_count = residual.shape[1]
    model_width = expert_gate_weight.shape[2]
    experts = lax.axis_size("route")
    capacity = 4 * length // experts
    cell_ids = token_expert_choices * capacity + token_slot_positions
    flat_cells = cell_ids.reshape(-1)
    owners = (
        jnp.full((experts * capacity,), length, jnp.int32)
        .at[flat_cells]
        .set(jnp.repeat(jnp.arange(length, dtype=jnp.int32), 2))
    )
    scales = (
        jnp.zeros((experts * capacity,), jnp.float32)
        .at[flat_cells]
        .set(router_choice_weight.reshape(-1))
    )
    full_x, full_g = (
        lax.all_gather(hidden_cols, "cuts", axis=1, tiled=True),
        lax.all_gather(cotangent, "cuts", axis=1, tiled=True),
    )
    token_part = fill_slots(full_x, owners).reshape(experts, capacity, model_width)
    grad_part = weighted_slots(full_g, owners, scales).reshape(experts, capacity, model_width)
    slot_x, slot_g = (
        lax.all_to_all(token_part, "route", split_axis=0, concat_axis=0, tiled=True),
        lax.all_to_all(grad_part, "route", split_axis=0, concat_axis=0, tiled=True),
    )
    expert_input_rows = slot_x.reshape(-1, model_width)
    rows_g = slot_g.reshape(-1, model_width)
    reduce_final_axis = (((1,), (1,)), ((), ()))
    contract_first = (((0,), (0,)), ((), ()))
    gate_primary_product = lax.dot_general(
        expert_input_rows,
        expert_gate_weight[0],
        reduce_final_axis,
        preferred_element_type=jnp.float32,
    )
    adapter_product = lax.dot_general(
        expert_input_rows,
        adapter_down_factor[0],
        reduce_final_axis,
        preferred_element_type=jnp.float32,
    ).astype(jnp.bfloat16)
    gate_preactivation = gate_primary_product + ADAPTER_SCALE * jnp.dot(
        adapter_product, adapter_up_factor[0], preferred_element_type=jnp.float32
    )
    sigmoid_gate = jax.nn.sigmoid(gate_preactivation)
    activ = (gate_preactivation * sigmoid_gate).astype(jnp.bfloat16)
    partial_out = jnp.dot(activ, expert_down_weight[0], preferred_element_type=jnp.float32).astype(
        jnp.bfloat16
    )
    slot_sums = lax.psum_scatter(
        partial_out.astype(jnp.float32)
        .reshape(experts, capacity, model_width)
        .astype(jnp.bfloat16),
        "cuts",
        scatter_dimension=2,
        tiled=True,
    ).astype(jnp.float32)
    returned = (
        lax.all_to_all(
            slot_sums.astype(jnp.bfloat16), "route", split_axis=0, concat_axis=0, tiled=True
        )
        .astype(slot_sums.dtype)
        .reshape(experts * capacity, col_count)
    )
    merged = hidden_cols.astype(jnp.float32) + combine_rows(
        returned, cell_ids, router_choice_weight
    )
    layer_out = merged.astype(jnp.bfloat16)
    grad_hidden = lax.dot_general(
        rows_g, expert_down_weight[0], reduce_final_axis, preferred_element_type=jnp.float32
    )
    preactivation_gradient = (
        grad_hidden * sigmoid_gate * (1.0 + gate_preactivation * (1.0 - sigmoid_gate))
    ).astype(jnp.bfloat16)
    up_factor_gradient = ADAPTER_SCALE * lax.dot_general(
        adapter_product, preactivation_gradient, contract_first, preferred_element_type=jnp.float32
    )
    factor_part = lax.dot_general(
        preactivation_gradient,
        adapter_up_factor[0],
        reduce_final_axis,
        preferred_element_type=jnp.float32,
    ).astype(jnp.bfloat16)
    gradient_pieces = lax.dot_general(
        factor_part, expert_input_rows, contract_first, preferred_element_type=jnp.float32
    )
    down_factor_gradient = ADAPTER_SCALE * lax.psum_scatter(
        gradient_pieces.astype(jnp.bfloat16), "cuts", scatter_dimension=1, tiled=True
    ).astype(jnp.float32)
    return (layer_out, down_factor_gradient[None], up_factor_gradient[None])


def local(*arrays):
    choices, positions = 6, 7
    length, experts = arrays[choices].shape[0], lax.axis_size("route")
    if 4 * length // experts >= length:
        return dense_layer(*arrays[:positions], *arrays[positions + 1 :])
    return slot_layer(*arrays)


def solution(mesh):
    return jax.shard_map(
        local,
        mesh=mesh,
        in_specs=(
            P(("group", "route"), "cuts"),
            P(("group", "route"), "cuts"),
            P(("group", "route"), "cuts"),
            P("cuts", None),
            P(("group", "route"), "cuts"),
            P(("group", "route"), "cuts"),
            P(("group", "route"), None),
            P(("group", "route"), None),
            P(("group", "route"), None),
            P("route", "cuts", None),
            P("route", "cuts", None),
            P("route", None, None),
            P("route", None, "cuts"),
        ),
        out_specs=(
            P(("group", "route"), "cuts"),
            P(("group", "route"), None, "cuts"),
            P(("group", "route"), None, "cuts"),
        ),
        check_vma=False,
    )
```

```python
import functools
import math

import jax
import jax.numpy as jnp
from jax import lax
from jax.experimental import pallas as pl
from jax.experimental.pallas import tpu as pltpu
from jax.sharding import PartitionSpec as P

HEAD_DIM = 128
ADAPTER_SCALE = 0.5
F32 = jnp.float32
BF16 = jnp.bfloat16
LAST = (((1,), (1,)), ((), ()))
FIRST = (((0,), (0,)), ((), ()))


def fetch(blocks, w_hbm, wbuf, sems):
    copies = []
    for i, block in enumerate(blocks):
        width = wbuf.shape[2]
        columns = pl.ds(pl.multiple_of(block * width, width), width)
        copies.append(pltpu.make_async_copy(w_hbm.at[:, columns], wbuf.at[i], sems.at[i]))
        copies[-1].start()
    return copies


def attend_kernel(across, q_ref, k_ref, v_ref, w_hbm, att, out, wbuf, sems):
    (copy,) = fetch(across.blocks()[-1:], w_hbm, wbuf, sems)
    length = q_ref.shape[0]
    per_kv = q_ref.shape[1] // k_ref.shape[1]
    rows = per_kv * length
    query_at = lax.broadcasted_iota(jnp.int32, (rows, length), 0) % length
    future = lax.broadcasted_iota(jnp.int32, (rows, length), 1) > query_at
    for g in range(k_ref.shape[1] // HEAD_DIM):
        lanes = slice(g * HEAD_DIM, (g + 1) * HEAD_DIM)
        heads = [
            slice((g * per_kv + h) * HEAD_DIM, (g * per_kv + h + 1) * HEAD_DIM) for h in range(per_kv)
        ]
        queries = jnp.concatenate([q_ref[:, h] for h in heads], axis=0)
        scores = lax.dot_general(queries, k_ref[:, lanes], LAST, preferred_element_type=F32)
        scores = jnp.where(future, -jnp.inf, scores * (1.0 / math.sqrt(HEAD_DIM)))
        shifted = jnp.exp(scores - jnp.max(scores, axis=-1, keepdims=True))
        weights = (shifted / jnp.sum(shifted, axis=-1, keepdims=True)).astype(BF16)
        got = jnp.dot(weights, v_ref[:, lanes], preferred_element_type=F32).astype(BF16)
        for i, h in enumerate(heads):
            att[:, h] = got[i * length : (i + 1) * length]
    copy.wait()
    out[...] = jnp.dot(att[...], wbuf[0], preferred_element_type=F32).astype(out.dtype)


def project_kernel(across, slots, att, r_ref, w_hbm, *refs):
    outs, (wbuf, sems) = refs[:-2], refs[-2:]
    blocks = across.blocks()
    copies = fetch([blocks[m] for m in slots], w_hbm, wbuf, sems)
    for i, m in enumerate(slots):
        copies[i].wait()
        term = jnp.dot(att[...], wbuf[i], preferred_element_type=F32)
        if m == 0:
            term = term + r_ref[...].astype(F32)
        outs[i][...] = term.astype(outs[i].dtype)


def projecting(kernel, outs, args, matrix, slots, width, flops):
    whole = pl.BlockSpec(memory_space=pltpu.VMEM)
    shapes = [jax.ShapeDtypeStruct(shape, dtype) for shape, dtype in outs]
    return pl.pallas_call(
        kernel,
        out_shape=shapes,
        in_specs=[whole] * len(args) + [pl.BlockSpec(memory_space=pl.ANY)],
        out_specs=[whole] * len(outs),
        scratch_shapes=[
            pltpu.VMEM((slots, matrix.shape[0], width), BF16),
            pltpu.SemaphoreType.DMA((slots,)),
        ],
        cost_estimate=pl.CostEstimate(
            flops=flops, bytes_accessed=2 * slots * matrix.shape[0] * width, transcendentals=0
        ),
    )(*args, matrix)


def attend_and_project(across, queries, keys, values, residual, matrix):
    length, width = residual.shape
    rows = (length, queries.shape[1])
    one = 2 * length * queries.shape[1] * width
    attended, last = projecting(
        functools.partial(attend_kernel, across),
        [(rows, BF16), ((length, width), BF16)],
        [queries, keys, values],
        matrix,
        1,
        width,
        one + 4 * length * length * queries.shape[1],
    )
    slots = list(range(across.n - 1))[::-1]
    others = projecting(
        functools.partial(project_kernel, across, slots),
        [((length, width), F32 if m == 0 else BF16) for m in slots],
        [attended, residual],
        matrix,
        len(slots),
        width,
        one * len(slots),
    )
    return [*others[::-1], last]


class Swaps:
    def __init__(self, axis, n, stride=1):
        self.axis, self.n, self.stride = axis, n, stride

    def blocks(self):
        me = lax.axis_index(self.axis) // self.stride % self.n
        return [me ^ m for m in range(self.n)]

    def swap(self, x, bit):
        step = bit * self.stride
        pairs = [(i, i ^ step) for i in range(lax.axis_size(self.axis))]
        return lax.ppermute(x, self.axis, pairs)

    def gather(self, x, highest=False):
        slots = [x]
        for m in range(1, self.n):
            bit = 1 << m.bit_length() - 1 if highest else m & -m
            slots.append(self.swap(slots[m ^ bit], bit))
        return slots

    def reduce(self, slots):
        sums = [[x] for x in slots]
        for m in reversed(range(1, self.n)):
            term = sums[m][0]
            for x in sums[m][1:]:
                term = term.astype(F32) + x.astype(F32)
            sums[m & (m - 1)].append(self.swap(term.astype(BF16), m & -m))
        return sum((x.astype(F32) for x in sums[0][1:]), sums[0][0].astype(F32))


def column_block(matrix, block, width):
    return lax.dynamic_slice_in_dim(matrix, block * width, width, axis=1)


def dense_layer(
    query_matrix_rows,
    key_matrix_rows,
    value_matrix_rows,
    attention_output_matrix,
    residual,
    cotangent,
    token_expert_choices,
    router_choice_weight,
    expert_gate_weight,
    expert_down_weight,
    adapter_down_factor,
    adapter_up_factor,
):
    width = residual.shape[1]
    cuts, route = lax.axis_size("cuts"), lax.axis_size("route")
    inner = min(2, route)
    across = Swaps("cuts", cuts)
    chips = Swaps("route", route // inner, inner)
    cores = Swaps("route", inner)

    def spread(x):
        mine = jnp.concatenate(chips.gather(x), axis=0)
        return cores.gather(mine)

    def collect(parts):
        own = cores.reduce(parts).astype(BF16)
        return chips.reduce(jnp.split(own, route // inner, axis=0)).astype(BF16)

    columns = across.blocks()
    gate, down = expert_gate_weight[0], expert_down_weight[0]
    low_in, low_out = adapter_down_factor[0], adapter_up_factor[0]

    chosen = token_expert_choices[:, :, None] == jnp.arange(route, dtype=jnp.int32)
    table = jnp.sum(jnp.where(chosen, router_choice_weight[:, :, None], 0.0), axis=1).T
    scales = [
        lax.dynamic_index_in_dim(x, lax.axis_index("route"), axis=1, keepdims=False).reshape(-1, 1)
        for x in spread(table[None])
    ]

    even = {0: cotangent}
    for m in range(2, cuts, 2):
        even[m] = across.swap(even[m & (m - 1)], m & -m)
    even = {m: jnp.concatenate(chips.gather(x), axis=0) for m, x in even.items()}
    cot_slots = {m: cores.gather(x) for m, x in even.items()}
    if cuts > 1:
        odd = cores.gather(across.swap(jnp.concatenate(list(even.values()), axis=0), 1))
        odd = [jnp.split(x, cuts // 2, axis=0) for x in odd]
        for i, m in enumerate(even):
            cot_slots[m + 1] = [x[i] for x in odd]

    terms = attend_and_project(
        across,
        query_matrix_rows,
        key_matrix_rows,
        value_matrix_rows,
        residual,
        attention_output_matrix,
    )
    hidden = across.reduce(terms).astype(BF16)
    hid_slots = [spread(x) for x in across.gather(hidden)]

    halves = range(inner)
    pre, low, grad_hidden = ([0.0] * inner for _ in range(3))
    for m in sorted(range(cuts), key=lambda m: (m % 2, m)):
        if m == cuts - 1:
            pre, low = lax.optimization_barrier((pre, low))
        if m == 1:
            grad_hidden = lax.optimization_barrier(grad_hidden)
        for h in halves:
            grad_hidden[h] += lax.dot_general(
                cot_slots[m][h], column_block(down, columns[m], width), LAST, preferred_element_type=F32
            )
            pre[h] += lax.dot_general(
                hid_slots[m][h], column_block(gate, columns[m], width), LAST, preferred_element_type=F32
            )
            low[h] += lax.dot_general(
                hid_slots[m][h], column_block(low_in, columns[m], width), LAST, preferred_element_type=F32
            )
    activ = [0.0] * inner
    for h in halves:
        low[h] = low[h].astype(BF16)
        pre[h] += ADAPTER_SCALE * jnp.dot(low[h], low_out, preferred_element_type=F32)
        activ[h] = (pre[h] * jax.nn.sigmoid(pre[h])).astype(BF16)

    outs = [None] * cuts
    for m in reversed(range(cuts)):
        parts = []
        for h in halves:
            part = jnp.dot(
                activ[h], column_block(down, columns[m], width), preferred_element_type=F32
            )
            parts.append((scales[h] * part).astype(BF16))
        if m == cuts - 1:
            pre, parts = lax.optimization_barrier((pre, parts))
        outs[m] = collect(parts)
    layer_out = (hidden.astype(F32) + across.reduce(outs)).astype(BF16)

    up_grad, factors = 0.0, []
    for h in halves:
        sig = jax.nn.sigmoid(pre[h])
        slope = sig * (1.0 + pre[h] * (1.0 - sig))
        grad_pre = (scales[h] * grad_hidden[h] * slope).astype(BF16)
        up_grad += lax.dot_general(low[h], grad_pre, FIRST, preferred_element_type=F32)
        factors.append(
            lax.dot_general(low_out, grad_pre, LAST, preferred_element_type=F32).astype(BF16)
        )
    up_grad = ADAPTER_SCALE * up_grad
    factor = jnp.concatenate(factors, axis=0)
    shift = 1
    while shift < cuts:
        other = across.swap(factor, shift)
        factor = (factor.astype(F32) + other.astype(F32)).astype(BF16)
        shift *= 2
    down_grad = ADAPTER_SCALE * sum(
        jnp.dot(x, rows, preferred_element_type=F32)
        for x, rows in zip(jnp.split(factor, inner, axis=0), hid_slots[0], strict=True)
    )
    return layer_out, down_grad[None], up_grad[None]


def causal_heads(query_matrix_rows, key_matrix_rows, value_matrix_rows):
    length = query_matrix_rows.shape[0]
    kv_local = key_matrix_rows.shape[1] // HEAD_DIM
    per_kv = query_matrix_rows.shape[1] // key_matrix_rows.shape[1]
    queries = query_matrix_rows.reshape(length, kv_local, per_kv, HEAD_DIM)
    key_view = key_matrix_rows.reshape(length, kv_local, HEAD_DIM)
    value_view = value_matrix_rows.reshape(length, kv_local, HEAD_DIM)
    scores = jnp.einsum(
        "qhgd,khd->hgqk", queries, key_view, preferred_element_type=jnp.float32
    ) / math.sqrt(HEAD_DIM)
    future = lax.broadcasted_iota(jnp.int32, (length, length), 1) > lax.broadcasted_iota(
        jnp.int32, (length, length), 0
    )
    scores = jnp.where(future, -jnp.inf, scores)
    row_max = jnp.max(scores, axis=-1, keepdims=True)
    shifted = jnp.exp(scores - row_max)
    weights = (shifted / jnp.sum(shifted, axis=-1, keepdims=True)).astype(jnp.bfloat16)
    attended = jnp.einsum("hgqk,khd->qhgd", weights, value_view, preferred_element_type=jnp.float32)
    return attended.astype(jnp.bfloat16).reshape(length, query_matrix_rows.shape[1])


def fill_slots(source_rows, owners):
    padded = jnp.concatenate(
        [source_rows, jnp.zeros((1, source_rows.shape[1]), source_rows.dtype)], axis=0
    )
    return jnp.take(padded, owners, axis=0)


def weighted_slots(source_rows, owners, scales):
    return (fill_slots(source_rows, owners).astype(jnp.float32) * scales[:, None]).astype(
        jnp.bfloat16
    )


def combine_rows(returned, cell_ids, router_choice_weight):
    first_out = jnp.take(returned, cell_ids[:, 0], axis=0)
    second_out = jnp.take(returned, cell_ids[:, 1], axis=0)
    return router_choice_weight[:, 0:1] * first_out + router_choice_weight[:, 1:2] * second_out


def slot_layer(
    query_matrix_rows,
    key_matrix_rows,
    value_matrix_rows,
    attention_output_matrix,
    residual,
    cotangent,
    token_expert_choices,
    token_slot_positions,
    router_choice_weight,
    expert_gate_weight,
    expert_down_weight,
    adapter_down_factor,
    adapter_up_factor,
):
    attended = causal_heads(query_matrix_rows, key_matrix_rows, value_matrix_rows)
    head_terms = jnp.dot(attended, attention_output_matrix, preferred_element_type=jnp.float32)
    head_cols = lax.psum_scatter(head_terms, "cuts", scatter_dimension=1, tiled=True)
    hidden_cols = (residual.astype(jnp.float32) + head_cols).astype(jnp.bfloat16)
    length = residual.shape[0]
    col_count = residual.shape[1]
    model_width = expert_gate_weight.shape[2]
    experts = lax.axis_size("route")
    capacity = 4 * length // experts
    cell_ids = token_expert_choices * capacity + token_slot_positions
    flat_cells = cell_ids.reshape(-1)
    owners = (
        jnp.full((experts * capacity,), length, jnp.int32)
        .at[flat_cells]
        .set(jnp.repeat(jnp.arange(length, dtype=jnp.int32), 2))
    )
    scales = (
        jnp.zeros((experts * capacity,), jnp.float32)
        .at[flat_cells]
        .set(router_choice_weight.reshape(-1))
    )
    full_x, full_g = (
        lax.all_gather(hidden_cols, "cuts", axis=1, tiled=True),
        lax.all_gather(cotangent, "cuts", axis=1, tiled=True),
    )
    token_part = fill_slots(full_x, owners).reshape(experts, capacity, model_width)
    grad_part = weighted_slots(full_g, owners, scales).reshape(experts, capacity, model_width)
    slot_x, slot_g = (
        lax.all_to_all(token_part, "route", split_axis=0, concat_axis=0, tiled=True),
        lax.all_to_all(grad_part, "route", split_axis=0, concat_axis=0, tiled=True),
    )
    expert_input_rows = slot_x.reshape(-1, model_width)
    rows_g = slot_g.reshape(-1, model_width)
    reduce_final_axis = (((1,), (1,)), ((), ()))
    contract_first = (((0,), (0,)), ((), ()))
    gate_primary_product = lax.dot_general(
        expert_input_rows,
        expert_gate_weight[0],
        reduce_final_axis,
        preferred_element_type=jnp.float32,
    )
    adapter_product = lax.dot_general(
        expert_input_rows,
        adapter_down_factor[0],
        reduce_final_axis,
        preferred_element_type=jnp.float32,
    ).astype(jnp.bfloat16)
    gate_preactivation = gate_primary_product + ADAPTER_SCALE * jnp.dot(
        adapter_product, adapter_up_factor[0], preferred_element_type=jnp.float32
    )
    sigmoid_gate = jax.nn.sigmoid(gate_preactivation)
    activ = (gate_preactivation * sigmoid_gate).astype(jnp.bfloat16)
    partial_out = jnp.dot(activ, expert_down_weight[0], preferred_element_type=jnp.float32).astype(
        jnp.bfloat16
    )
    slot_sums = lax.psum_scatter(
        partial_out.astype(jnp.float32)
        .reshape(experts, capacity, model_width)
        .astype(jnp.bfloat16),
        "cuts",
        scatter_dimension=2,
        tiled=True,
    ).astype(jnp.float32)
    returned = (
        lax.all_to_all(
            slot_sums.astype(jnp.bfloat16), "route", split_axis=0, concat_axis=0, tiled=True
        )
        .astype(slot_sums.dtype)
        .reshape(experts * capacity, col_count)
    )
    merged = hidden_cols.astype(jnp.float32) + combine_rows(
        returned, cell_ids, router_choice_weight
    )
    layer_out = merged.astype(jnp.bfloat16)
    grad_hidden = lax.dot_general(
        rows_g, expert_down_weight[0], reduce_final_axis, preferred_element_type=jnp.float32
    )
    preactivation_gradient = (
        grad_hidden * sigmoid_gate * (1.0 + gate_preactivation * (1.0 - sigmoid_gate))
    ).astype(jnp.bfloat16)
    up_factor_gradient = ADAPTER_SCALE * lax.dot_general(
        adapter_product, preactivation_gradient, contract_first, preferred_element_type=jnp.float32
    )
    factor_part = lax.dot_general(
        preactivation_gradient,
        adapter_up_factor[0],
        reduce_final_axis,
        preferred_element_type=jnp.float32,
    ).astype(jnp.bfloat16)
    gradient_pieces = lax.dot_general(
        factor_part, expert_input_rows, contract_first, preferred_element_type=jnp.float32
    )
    down_factor_gradient = ADAPTER_SCALE * lax.psum_scatter(
        gradient_pieces.astype(jnp.bfloat16), "cuts", scatter_dimension=1, tiled=True
    ).astype(jnp.float32)
    return (layer_out, down_factor_gradient[None], up_factor_gradient[None])


def local(*arrays):
    choices, positions = 6, 7
    length, experts = arrays[choices].shape[0], lax.axis_size("route")
    powers = all(n & (n - 1) == 0 for n in (experts, lax.axis_size("cuts")))
    if powers and 4 * length // experts >= length:
        return dense_layer(*arrays[:positions], *arrays[positions + 1 :])
    return slot_layer(*arrays)


def solution(mesh):
    return jax.shard_map(
        local,
        mesh=mesh,
        in_specs=(
            P(("group", "route"), "cuts"),
            P(("group", "route"), "cuts"),
            P(("group", "route"), "cuts"),
            P("cuts", None),
            P(("group", "route"), "cuts"),
            P(("group", "route"), "cuts"),
            P(("group", "route"), None),
            P(("group", "route"), None),
            P(("group", "route"), None),
            P("route", "cuts", None),
            P("route", "cuts", None),
            P("route", None, None),
            P("route", None, "cuts"),
        ),
        out_specs=(
            P(("group", "route"), "cuts"),
            P(("group", "route"), None, "cuts"),
            P(("group", "route"), None, "cuts"),
        ),
        check_vma=False,
    )
```

```python
import functools
import math

import jax
import jax.numpy as jnp
from jax import lax
from jax.experimental import pallas as pl
from jax.experimental.pallas import tpu as pltpu
from jax.sharding import PartitionSpec as P

HEAD_DIM = 128
ADAPTER_SCALE = 0.5
F32 = jnp.float32
BF16 = jnp.bfloat16
COPY_PIECES = 8
LAST = (((1,), (1,)), ((), ()))
FIRST = (((0,), (0,)), ((), ()))


def fetch(blocks, w_hbm, wbuf, sems):
    copies = []
    pieces, (_, depth, width) = sems.shape[1], wbuf.shape
    for i, block in enumerate(blocks):
        columns = pl.ds(pl.multiple_of(block * width, width), width)
        copies.append([])
        for j in range(pieces):
            rows = pl.ds(j * (depth // pieces), depth // pieces)
            copy = pltpu.make_async_copy(
                w_hbm.at[rows, columns], wbuf.at[i, rows], sems.at[i, j]
            )
            copy.start()
            copies[i].append(copy)
    return copies


def attend_kernel(across, q_ref, k_ref, v_ref, w_hbm, att, out, wbuf, sems):
    (copies,) = fetch(across.blocks()[-1:], w_hbm, wbuf, sems)
    length = q_ref.shape[0]
    per_kv = q_ref.shape[1] // k_ref.shape[1]
    rows = per_kv * length
    query_at = lax.broadcasted_iota(jnp.int32, (rows, length), 0) % length
    future = lax.broadcasted_iota(jnp.int32, (rows, length), 1) > query_at
    for g in range(k_ref.shape[1] // HEAD_DIM):
        lanes = slice(g * HEAD_DIM, (g + 1) * HEAD_DIM)
        heads = [
            slice((g * per_kv + h) * HEAD_DIM, (g * per_kv + h + 1) * HEAD_DIM) for h in range(per_kv)
        ]
        queries = jnp.concatenate([q_ref[:, h] for h in heads], axis=0)
        scores = lax.dot_general(queries, k_ref[:, lanes], LAST, preferred_element_type=F32)
        scores = jnp.where(future, -jnp.inf, scores * (1.0 / math.sqrt(HEAD_DIM)))
        shifted = jnp.exp(scores - jnp.max(scores, axis=-1, keepdims=True))
        weights = (shifted / jnp.sum(shifted, axis=-1, keepdims=True)).astype(BF16)
        got = jnp.dot(weights, v_ref[:, lanes], preferred_element_type=F32).astype(BF16)
        for i, h in enumerate(heads):
            att[:, h] = got[i * length : (i + 1) * length]
    for copy in copies:
        copy.wait()
    out[...] = jnp.dot(att[...], wbuf[0], preferred_element_type=F32).astype(out.dtype)


def project_kernel(across, slots, att, r_ref, w_hbm, *refs):
    outs, (wbuf, sems) = refs[:-2], refs[-2:]
    blocks = across.blocks()
    copies = fetch([blocks[m] for m in slots], w_hbm, wbuf, sems)
    for i, m in enumerate(slots):
        for copy in copies[i]:
            copy.wait()
        term = jnp.dot(att[...], wbuf[i], preferred_element_type=F32)
        if m == 0:
            term = term + r_ref[...].astype(F32)
        outs[i][...] = term.astype(outs[i].dtype)


def projecting(kernel, outs, args, matrix, slots, width, flops):
    whole = pl.BlockSpec(memory_space=pltpu.VMEM)
    shapes = [pltpu.VMEM(shape, dtype) for shape, dtype in outs]
    return pl.pallas_call(
        kernel,
        out_shape=shapes,
        in_specs=[whole] * len(args) + [pl.BlockSpec(memory_space=pl.ANY)],
        out_specs=[whole] * len(outs),
        scratch_shapes=[
            pltpu.VMEM((slots, matrix.shape[0], width), BF16),
            pltpu.SemaphoreType.DMA((slots, COPY_PIECES)),
        ],
        cost_estimate=pl.CostEstimate(
            flops=flops, bytes_accessed=2 * slots * matrix.shape[0] * width, transcendentals=0
        ),
    )(*args, matrix)


def attend_and_project(across, queries, keys, values, residual, matrix):
    length, width = residual.shape
    rows = (length, queries.shape[1])
    one = 2 * length * queries.shape[1] * width
    attended, last = projecting(
        functools.partial(attend_kernel, across),
        [(rows, BF16), ((length, width), BF16)],
        [queries, keys, values],
        matrix,
        1,
        width,
        one + 4 * length * length * queries.shape[1],
    )
    slots = list(range(across.n - 1))[::-1]
    others = projecting(
        functools.partial(project_kernel, across, slots),
        [((length, width), F32 if m == 0 else BF16) for m in slots],
        [attended, residual],
        matrix,
        len(slots),
        width,
        one * len(slots),
    )
    return [*others[::-1], last]


class Swaps:
    def __init__(self, axis, n, stride=1):
        self.axis, self.n, self.stride = axis, n, stride

    def blocks(self):
        me = lax.axis_index(self.axis) // self.stride % self.n
        return [me ^ m for m in range(self.n)]

    def swap(self, x, bit):
        step = bit * self.stride
        pairs = [(i, i ^ step) for i in range(lax.axis_size(self.axis))]
        return lax.ppermute(x, self.axis, pairs)

    def gather(self, x, highest=False):
        slots = [x]
        for m in range(1, self.n):
            bit = 1 << m.bit_length() - 1 if highest else m & -m
            slots.append(self.swap(slots[m ^ bit], bit))
        return slots

    def reduce(self, slots):
        sums = [[x] for x in slots]
        for m in reversed(range(1, self.n)):
            term = sums[m][0]
            for x in sums[m][1:]:
                term = term.astype(F32) + x.astype(F32)
            sums[m & (m - 1)].append(self.swap(term.astype(BF16), m & -m))
        return sum((x.astype(F32) for x in sums[0][1:]), sums[0][0].astype(F32))


def column_block(matrix, block, width):
    return lax.dynamic_slice_in_dim(matrix, block * width, width, axis=1)


def dense_layer(
    query_matrix_rows,
    key_matrix_rows,
    value_matrix_rows,
    attention_output_matrix,
    residual,
    cotangent,
    token_expert_choices,
    router_choice_weight,
    expert_gate_weight,
    expert_down_weight,
    adapter_down_factor,
    adapter_up_factor,
):
    width = residual.shape[1]
    cuts, route = lax.axis_size("cuts"), lax.axis_size("route")
    inner = min(2, route)
    across = Swaps("cuts", cuts)
    chips = Swaps("route", route // inner, inner)
    cores = Swaps("route", inner)

    def spread(x):
        mine = jnp.concatenate(chips.gather(x), axis=0)
        return cores.gather(mine)

    def collect(parts):
        own = cores.reduce(parts).astype(BF16)
        return chips.reduce(jnp.split(own, route // inner, axis=0)).astype(BF16)

    columns = across.blocks()
    gate, down = expert_gate_weight[0], expert_down_weight[0]
    low_in, low_out = adapter_down_factor[0], adapter_up_factor[0]

    chosen = token_expert_choices[:, :, None] == jnp.arange(route, dtype=jnp.int32)
    table = jnp.sum(jnp.where(chosen, router_choice_weight[:, :, None], 0.0), axis=1).T
    scales = [
        lax.dynamic_index_in_dim(x, lax.axis_index("route"), axis=1, keepdims=False).reshape(-1, 1)
        for x in spread(table[None])
    ]

    even = {0: cotangent}
    for m in range(2, cuts, 2):
        even[m] = across.swap(even[m & (m - 1)], m & -m)
    even = {m: jnp.concatenate(chips.gather(x), axis=0) for m, x in even.items()}
    cot_slots = {m: cores.gather(x) for m, x in even.items()}
    if cuts > 1:
        odd = cores.gather(across.swap(jnp.concatenate(list(even.values()), axis=0), 1))
        odd = [jnp.split(x, cuts // 2, axis=0) for x in odd]
        for i, m in enumerate(even):
            cot_slots[m + 1] = [x[i] for x in odd]

    terms = attend_and_project(
        across,
        query_matrix_rows,
        key_matrix_rows,
        value_matrix_rows,
        residual,
        attention_output_matrix,
    )
    hidden = across.reduce(terms).astype(BF16)
    hid_slots = [spread(x) for x in across.gather(hidden)]

    halves = range(inner)
    pre, low, grad_hidden = ([0.0] * inner for _ in range(3))
    for m in sorted(range(cuts), key=lambda m: (m % 2, m)):
        if m == cuts - 1:
            pre, low = lax.optimization_barrier((pre, low))
        if m == 1:
            grad_hidden = lax.optimization_barrier(grad_hidden)
        for h in halves:
            grad_hidden[h] += lax.dot_general(
                cot_slots[m][h], column_block(down, columns[m], width), LAST, preferred_element_type=F32
            )
            pre[h] += lax.dot_general(
                hid_slots[m][h], column_block(gate, columns[m], width), LAST, preferred_element_type=F32
            )
            low[h] += lax.dot_general(
                hid_slots[m][h], column_block(low_in, columns[m], width), LAST, preferred_element_type=F32
            )
    activ = [0.0] * inner
    for h in halves:
        low[h] = low[h].astype(BF16)
        pre[h] += ADAPTER_SCALE * jnp.dot(low[h], low_out, preferred_element_type=F32)
        activ[h] = (pre[h] * jax.nn.sigmoid(pre[h])).astype(BF16)

    outs = [None] * cuts
    for m in reversed(range(cuts)):
        parts = []
        for h in halves:
            part = jnp.dot(
                activ[h], column_block(down, columns[m], width), preferred_element_type=F32
            )
            parts.append((scales[h] * part).astype(BF16))
        if m == cuts - 1:
            pre, parts = lax.optimization_barrier((pre, parts))
        outs[m] = collect(parts)
    layer_out = (hidden.astype(F32) + across.reduce(outs)).astype(BF16)

    up_grad, factors = 0.0, []
    for h in halves:
        sig = jax.nn.sigmoid(pre[h])
        slope = sig * (1.0 + pre[h] * (1.0 - sig))
        grad_pre = (scales[h] * grad_hidden[h] * slope).astype(BF16)
        up_grad += lax.dot_general(low[h], grad_pre, FIRST, preferred_element_type=F32)
        factors.append(
            lax.dot_general(low_out, grad_pre, LAST, preferred_element_type=F32).astype(BF16)
        )
    up_grad = ADAPTER_SCALE * up_grad
    factor = jnp.concatenate(factors, axis=0)
    shift = 1
    while shift < cuts:
        other = across.swap(factor, shift)
        factor = (factor.astype(F32) + other.astype(F32)).astype(BF16)
        shift *= 2
    down_grad = ADAPTER_SCALE * sum(
        jnp.dot(x, rows, preferred_element_type=F32)
        for x, rows in zip(jnp.split(factor, inner, axis=0), hid_slots[0], strict=True)
    )
    return layer_out, down_grad[None], up_grad[None]


def causal_heads(query_matrix_rows, key_matrix_rows, value_matrix_rows):
    length = query_matrix_rows.shape[0]
    kv_local = key_matrix_rows.shape[1] // HEAD_DIM
    per_kv = query_matrix_rows.shape[1] // key_matrix_rows.shape[1]
    queries = query_matrix_rows.reshape(length, kv_local, per_kv, HEAD_DIM)
    key_view = key_matrix_rows.reshape(length, kv_local, HEAD_DIM)
    value_view = value_matrix_rows.reshape(length, kv_local, HEAD_DIM)
    scores = jnp.einsum(
        "qhgd,khd->hgqk", queries, key_view, preferred_element_type=jnp.float32
    ) / math.sqrt(HEAD_DIM)
    future = lax.broadcasted_iota(jnp.int32, (length, length), 1) > lax.broadcasted_iota(
        jnp.int32, (length, length), 0
    )
    scores = jnp.where(future, -jnp.inf, scores)
    row_max = jnp.max(scores, axis=-1, keepdims=True)
    shifted = jnp.exp(scores - row_max)
    weights = (shifted / jnp.sum(shifted, axis=-1, keepdims=True)).astype(jnp.bfloat16)
    attended = jnp.einsum("hgqk,khd->qhgd", weights, value_view, preferred_element_type=jnp.float32)
    return attended.astype(jnp.bfloat16).reshape(length, query_matrix_rows.shape[1])


def fill_slots(source_rows, owners):
    padded = jnp.concatenate(
        [source_rows, jnp.zeros((1, source_rows.shape[1]), source_rows.dtype)], axis=0
    )
    return jnp.take(padded, owners, axis=0)


def weighted_slots(source_rows, owners, scales):
    return (fill_slots(source_rows, owners).astype(jnp.float32) * scales[:, None]).astype(
        jnp.bfloat16
    )


def combine_rows(returned, cell_ids, router_choice_weight):
    first_out = jnp.take(returned, cell_ids[:, 0], axis=0)
    second_out = jnp.take(returned, cell_ids[:, 1], axis=0)
    return router_choice_weight[:, 0:1] * first_out + router_choice_weight[:, 1:2] * second_out


def slot_layer(
    query_matrix_rows,
    key_matrix_rows,
    value_matrix_rows,
    attention_output_matrix,
    residual,
    cotangent,
    token_expert_choices,
    token_slot_positions,
    router_choice_weight,
    expert_gate_weight,
    expert_down_weight,
    adapter_down_factor,
    adapter_up_factor,
):
    attended = causal_heads(query_matrix_rows, key_matrix_rows, value_matrix_rows)
    head_terms = jnp.dot(attended, attention_output_matrix, preferred_element_type=jnp.float32)
    head_cols = lax.psum_scatter(head_terms, "cuts", scatter_dimension=1, tiled=True)
    hidden_cols = (residual.astype(jnp.float32) + head_cols).astype(jnp.bfloat16)
    length = residual.shape[0]
    col_count = residual.shape[1]
    model_width = expert_gate_weight.shape[2]
    experts = lax.axis_size("route")
    capacity = 4 * length // experts
    cell_ids = token_expert_choices * capacity + token_slot_positions
    flat_cells = cell_ids.reshape(-1)
    owners = (
        jnp.full((experts * capacity,), length, jnp.int32)
        .at[flat_cells]
        .set(jnp.repeat(jnp.arange(length, dtype=jnp.int32), 2))
    )
    scales = (
        jnp.zeros((experts * capacity,), jnp.float32)
        .at[flat_cells]
        .set(router_choice_weight.reshape(-1))
    )
    full_x, full_g = (
        lax.all_gather(hidden_cols, "cuts", axis=1, tiled=True),
        lax.all_gather(cotangent, "cuts", axis=1, tiled=True),
    )
    token_part = fill_slots(full_x, owners).reshape(experts, capacity, model_width)
    grad_part = weighted_slots(full_g, owners, scales).reshape(experts, capacity, model_width)
    slot_x, slot_g = (
        lax.all_to_all(token_part, "route", split_axis=0, concat_axis=0, tiled=True),
        lax.all_to_all(grad_part, "route", split_axis=0, concat_axis=0, tiled=True),
    )
    expert_input_rows = slot_x.reshape(-1, model_width)
    rows_g = slot_g.reshape(-1, model_width)
    reduce_final_axis = (((1,), (1,)), ((), ()))
    contract_first = (((0,), (0,)), ((), ()))
    gate_primary_product = lax.dot_general(
        expert_input_rows,
        expert_gate_weight[0],
        reduce_final_axis,
        preferred_element_type=jnp.float32,
    )
    adapter_product = lax.dot_general(
        expert_input_rows,
        adapter_down_factor[0],
        reduce_final_axis,
        preferred_element_type=jnp.float32,
    ).astype(jnp.bfloat16)
    gate_preactivation = gate_primary_product + ADAPTER_SCALE * jnp.dot(
        adapter_product, adapter_up_factor[0], preferred_element_type=jnp.float32
    )
    sigmoid_gate = jax.nn.sigmoid(gate_preactivation)
    activ = (gate_preactivation * sigmoid_gate).astype(jnp.bfloat16)
    partial_out = jnp.dot(activ, expert_down_weight[0], preferred_element_type=jnp.float32).astype(
        jnp.bfloat16
    )
    slot_sums = lax.psum_scatter(
        partial_out.astype(jnp.float32)
        .reshape(experts, capacity, model_width)
        .astype(jnp.bfloat16),
        "cuts",
        scatter_dimension=2,
        tiled=True,
    ).astype(jnp.float32)
    returned = (
        lax.all_to_all(
            slot_sums.astype(jnp.bfloat16), "route", split_axis=0, concat_axis=0, tiled=True
        )
        .astype(slot_sums.dtype)
        .reshape(experts * capacity, col_count)
    )
    merged = hidden_cols.astype(jnp.float32) + combine_rows(
        returned, cell_ids, router_choice_weight
    )
    layer_out = merged.astype(jnp.bfloat16)
    grad_hidden = lax.dot_general(
        rows_g, expert_down_weight[0], reduce_final_axis, preferred_element_type=jnp.float32
    )
    preactivation_gradient = (
        grad_hidden * sigmoid_gate * (1.0 + gate_preactivation * (1.0 - sigmoid_gate))
    ).astype(jnp.bfloat16)
    up_factor_gradient = ADAPTER_SCALE * lax.dot_general(
        adapter_product, preactivation_gradient, contract_first, preferred_element_type=jnp.float32
    )
    factor_part = lax.dot_general(
        preactivation_gradient,
        adapter_up_factor[0],
        reduce_final_axis,
        preferred_element_type=jnp.float32,
    ).astype(jnp.bfloat16)
    gradient_pieces = lax.dot_general(
        factor_part, expert_input_rows, contract_first, preferred_element_type=jnp.float32
    )
    down_factor_gradient = ADAPTER_SCALE * lax.psum_scatter(
        gradient_pieces.astype(jnp.bfloat16), "cuts", scatter_dimension=1, tiled=True
    ).astype(jnp.float32)
    return (layer_out, down_factor_gradient[None], up_factor_gradient[None])


def local(*arrays):
    choices, positions = 6, 7
    length, experts = arrays[choices].shape[0], lax.axis_size("route")
    powers = all(n & (n - 1) == 0 for n in (experts, lax.axis_size("cuts")))
    if powers and 4 * length // experts >= length:
        return dense_layer(*arrays[:positions], *arrays[positions + 1 :])
    return slot_layer(*arrays)


def solution(mesh):
    return jax.shard_map(
        local,
        mesh=mesh,
        in_specs=(
            P(("group", "route"), "cuts"),
            P(("group", "route"), "cuts"),
            P(("group", "route"), "cuts"),
            P("cuts", None),
            P(("group", "route"), "cuts"),
            P(("group", "route"), "cuts"),
            P(("group", "route"), None),
            P(("group", "route"), None),
            P(("group", "route"), None),
            P("route", "cuts", None),
            P("route", "cuts", None),
            P("route", None, None),
            P("route", None, "cuts"),
        ),
        out_specs=(
            P(("group", "route"), "cuts"),
            P(("group", "route"), None, "cuts"),
            P(("group", "route"), None, "cuts"),
        ),
        check_vma=False,
    )
```
